32 devices in a mesh: pb: 4 (over y, x), aux: 8 (over z, core).
Axes of the slice: x: 2, y: 2, z: 4, core: 2. Of those that a mesh axis runs over, the one named last changes fastest.
Arguments:
- ao_blocks: float32 [4, 4, 640, 2, 6400], P('pb', None, 'aux'), may hold values from -1 to 1
- occ_coef: float32 [27, 2, 80, 16], replicated, may hold values from -0.625 to 0.625
- vir_coef: float32 [27, 2, 80, 64], replicated, may hold values from -0.625 to 0.625
- occ_energy: float32 [27, 16], replicated, may hold values from -2.5 to -0.5
- vir_energy: float32 [27, 64], replicated, may hold values from 0.5 to 4
- kpoint_diff: int32 [27, 27], replicated, may hold values from 0 to 26, as said below
- transfer_label: int32 [4], replicated, may hold values from 1 to 26, as said below
- chosen_rows: int32 [4, 4], replicated, may hold values from 0 to 26, as said below
Outputs:
- amplitudes: float32 [4, 2, 2, 2, 16, 16, 4096], P('pb', None, None, None, 'aux')
The draws below stay inside these ranges and needn't reach their ends.
Inputs may be any that keep to these rules, and one draw needn't show every extreme that they name: The k-points are the points of a 3 x 3 x 3 periodic mesh under a relabeling drawn from the seed, with label 0 for the zero transfer; kpoint_diff[k, q] is the label of k - q modulo the mesh, so it is a group table. `transfer_label`: the labels are nonzero transfers, all different; slots 2m and 2m + 1 hold opposite transfers, q and -q. `chosen_rows`: the four entries of each row are different k labels.
All inputs are finite; a program needn't handle non-finite values.
Results may differ from the reference program's by a relative error of at most 0.0001.
Values sent between devices are 32-bit elements; how exact they have to be, the bound alone decides.
No kernel may reach another device: no remote copies, remote signals or barrier semaphores. Data moves between devices by JAX's collectives and lax.ppermute only.
A program may use at most 128 MiB of HBM per device.

```python
import jax
import jax.numpy as jnp
import numpy as np
from jax import lax

NK = 27
NOCC = 16
NVIR = 64
NAO = 80
NAUX = 640
Q = 4


def mesh_labels(key):
    rest = jax.random.permutation(jax.random.fold_in(key, 7), NK - 1).astype(jnp.int32) + 1
    return jnp.concatenate([jnp.zeros((1,), jnp.int32), rest]).astype(jnp.int32)


def negate_flat(flat_index):
    xpos = flat_index // 9
    ypos = flat_index // 3 % 3
    zpos = flat_index % 3
    return (3 - xpos) % 3 * 9 + (3 - ypos) % 3 * 3 + (3 - zpos) % 3


def draw_kpoint_diff(key, part):
    labels = mesh_labels(key)
    inverse = jnp.argsort(labels).astype(jnp.int32)
    first = inverse[:, None]
    second = inverse[None, :]
    xdiff = (first // 9 - second // 9) % 3
    ydiff = (first // 3 % 3 - second // 3 % 3) % 3
    zdiff = (first % 3 - second % 3) % 3
    return labels[xdiff * 9 + ydiff * 3 + zdiff].astype(jnp.int32)


def draw_transfer_label(key, part):
    labels = mesh_labels(key)
    inverse = jnp.argsort(labels).astype(jnp.int32)
    negs = np.array([(3 - f // 9) % 3 * 9 + (3 - f // 3 % 3) % 3 * 3 + (3 - f % 3) % 3 for f in range(27)])
    chosen = np.array([f for f in range(1, 27) if f < negs[f]], dtype=np.int32)
    chosen_arr = jnp.asarray(chosen)
    top_flat = inverse[NK - 1]
    top_rep = jnp.minimum(top_flat, negate_flat(top_flat))
    top_pos = jnp.sum((chosen_arr < top_rep).astype(jnp.int32)).astype(jnp.int32)
    order = jax.random.permutation(jax.random.fold_in(key, 11), 13).astype(jnp.int32)
    where_top = jnp.argmax((order == top_pos).astype(jnp.int32)).astype(jnp.int32)
    order = order.at[where_top].set(order[0]).at[0].set(top_pos)
    picked = chosen_arr[order[:Q // 2]]
    opposite = negate_flat(picked)
    pairs = jnp.stack([labels[picked], labels[opposite]], axis=1)
    return pairs.reshape(Q).astype(jnp.int32)


def draw_chosen_rows(key, part):
    keys = jax.random.split(jax.random.fold_in(key, 13), Q)
    return jax.vmap(lambda single: jax.random.permutation(single, NK)[:4])(keys).astype(jnp.int32)


def block_levels(own_key, extent, shards, low, high):
    gain = 1.0
    for dim, blocks in shards:
        heights = jax.random.uniform(jax.random.fold_in(jax.random.fold_in(own_key, 6), dim), (blocks,), jnp.float32, low / len(shards), high / len(shards))
        gain = gain * jnp.repeat(jnp.exp(heights), extent[dim] // blocks).reshape((-1,) + (1,) * (len(extent) - 1 - dim))
    return gain


def gaussian(rng, dims, scale, most, pieces=(), held_as=jnp.bfloat16):
    gain = block_levels(rng, dims, pieces, -0.22, 0.18) if pieces else 1.0
    values = jax.random.normal(rng, dims, jnp.float32) * scale * gain
    return jnp.minimum(jnp.maximum(values, -most), most).astype(held_as)


def setup_inputs(seed: int = 0) -> dict:
    seeds = jax.random.split(jax.random.key(seed), 9)
    return {
        "ao_blocks": gaussian(seeds[0], (Q, 4, NAUX, 2, NAO * NAO), (NAUX // 16) ** -0.5, 1.0, ((0, 4), (2, 8)), jnp.float32),
        "occ_coef": gaussian(seeds[1], (NK, 2, NAO, NOCC), NAO ** -0.5, 0.625, (), jnp.float32),
        "vir_coef": gaussian(seeds[2], (NK, 2, NAO, NVIR), NAO ** -0.5, 0.625, (), jnp.float32),
        "occ_energy": jnp.clip(jax.random.uniform(seeds[3], (NK, NOCC), jnp.float32, -2.5, -0.5), -2.5, -0.5),
        "vir_energy": jnp.clip(jax.random.uniform(seeds[4], (NK, NVIR), jnp.float32, 0.5, 4.0), 0.5, 4.0),
        "kpoint_diff": draw_kpoint_diff(jax.random.fold_in(seeds[8], 71), 0),
        "transfer_label": draw_transfer_label(jax.random.fold_in(seeds[8], 71), 0),
        "chosen_rows": draw_chosen_rows(jax.random.fold_in(seeds[8], 71), 0),
    }


def to_orbitals(blocks, occ_sel, vir_sel):
    highest = lax.Precision.HIGHEST
    ao_width = occ_sel.shape[2]
    complex_ao = blocks.reshape(blocks.shape[0], blocks.shape[1], 2, ao_width, ao_width)
    real_ao = complex_ao[:, :, 0]
    imag_ao = complex_ao[:, :, 1]
    occ_real = occ_sel[:, 0]
    occ_imag = occ_sel[:, 1]
    half_real = jnp.einsum('smi,spmn->spin', occ_real, real_ao, precision=highest) + jnp.einsum('smi,spmn->spin', occ_imag, imag_ao, precision=highest)
    half_imag = jnp.einsum('smi,spmn->spin', occ_real, imag_ao, precision=highest) - jnp.einsum('smi,spmn->spin', occ_imag, real_ao, precision=highest)
    vir_real = vir_sel[:, 0]
    vir_imag = vir_sel[:, 1]
    full_real = jnp.einsum('spin,sna->spia', half_real, vir_real, precision=highest) - jnp.einsum('spin,sna->spia', half_imag, vir_imag, precision=highest)
    full_imag = jnp.einsum('spin,sna->spia', half_real, vir_imag, precision=highest) + jnp.einsum('spin,sna->spia', half_imag, vir_real, precision=highest)
    return jnp.concatenate([full_real, full_imag], axis=3)


def pair_sums(left_side, right_side, vir_width):
    highest = lax.Precision.HIGHEST
    pattern = 'spia,tpjb->stijab'
    left_real = left_side[..., :vir_width]
    left_imag = left_side[..., vir_width:]
    right_real = right_side[..., :vir_width]
    right_imag = right_side[..., vir_width:]
    real_part = jnp.einsum(pattern, left_real, right_real, precision=highest) - jnp.einsum(pattern, left_imag, right_imag, precision=highest)
    imag_part = jnp.einsum(pattern, left_real, right_imag, precision=highest) + jnp.einsum(pattern, left_imag, right_real, precision=highest)
    return real_part, imag_part


def make_amplitudes(real_part, imag_part, occ_left, occ_right, vir_left, vir_right):
    denominator = (occ_left[:, None, :, None, None, None] + occ_right[None, :, None, :, None, None]
                   - vir_left[:, None, None, None, :, None] - vir_right[None, :, None, None, None, :])
    result = jnp.stack([real_part / denominator, imag_part / denominator])
    shape_now = result.shape
    return result.reshape(shape_now[0], shape_now[1], shape_now[2], shape_now[3], shape_now[4], shape_now[5] * shape_now[6])


def reference(ao_blocks, occ_coef, vir_coef, occ_energy, vir_energy, kpoint_diff, transfer_label, chosen_rows):
    vir_width = vir_coef.shape[3]
    orbitals = []
    for position in range(Q):
        own_rows = chosen_rows[position]
        own_vir = kpoint_diff[own_rows, transfer_label[position]]
        orbitals.append(to_orbitals(ao_blocks[position], occ_coef[own_rows], vir_coef[own_vir]))
    outputs = []
    for position in range(Q):
        partner = position ^ 1
        own_rows = chosen_rows[position]
        own_vir = kpoint_diff[own_rows, transfer_label[position]]
        other_rows = chosen_rows[partner]
        other_vir = kpoint_diff[other_rows, transfer_label[partner]]
        real_part, imag_part = pair_sums(orbitals[position][0:2], orbitals[partner][2:4], vir_width)
        outputs.append(make_amplitudes(real_part, imag_part, occ_energy[own_rows[0:2]], occ_energy[other_rows[2:4]],
                                       vir_energy[own_vir[0:2]], vir_energy[other_vir[2:4]]))
    return jnp.stack(outputs)
```

```python
import functools

import jax
import jax.numpy as jnp
from jax import lax
from jax.experimental import pallas as pl
from jax.experimental.pallas import tpu as pltpu
from jax.sharding import PartitionSpec as P

LANES = 128
F32 = jnp.float32
BF16 = jnp.bfloat16


def gcd(a, b):
    while b:
        a, b = b, a % b
    return a


def split(value):
    high = value.astype(BF16)
    low = (value - high.astype(F32)).astype(BF16)
    return high, low


def orbital_kernel(
    aux_all, slot_ref, rows_ref, diff_ref, label_ref, x_ref, occ_ref, vir_ref, o_ref, w_ref, c_ref, t_ref
):
    n_ao = occ_ref.shape[3]
    n_occ = occ_ref.shape[2]
    n_vir = vir_ref.shape[2]
    group = LANES // gcd(n_ao, LANES)
    tiles = n_ao * group // LANES
    aux_here = x_ref.shape[2]
    stretches = n_ao // group
    pairs = aux_here * stretches
    wide = 2 * n_vir
    step = pl.program_id(1)

    def covers(tile):
        return [r for r in range(group) if r * n_ao < (tile + 1) * LANES and (r + 1) * n_ao > tile * LANES]

    @pl.when(step == 0)
    def _():
        vir_real = jnp.transpose(vir_ref[0, 0], (1, 0))
        vir_imag = jnp.transpose(vir_ref[0, 1], (1, 0))
        of_real = jnp.concatenate([vir_real, vir_imag], axis=1)
        of_imag = jnp.concatenate([-vir_imag, vir_real], axis=1)
        w_ref[...] = jnp.zeros_like(w_ref)
        for part, both in enumerate((of_real, of_imag)):
            high, low = split(both)
            for tile in range(tiles):
                for place, r in enumerate(covers(tile)):
                    start = max(0, r * n_ao - tile * LANES)
                    stop = min(LANES, (r + 1) * n_ao - tile * LANES)
                    begin = tile * LANES + start - r * n_ao
                    for kind, piece in enumerate((high, low, high)):
                        row = kind * 2 * LANES + part * LANES + start
                        w_ref[tile, row : row + stop - start, place * wide : (place + 1) * wide] = piece[
                            begin : begin + stop - start
                        ]
        both = jnp.concatenate([occ_ref[0, 0], occ_ref[0, 1]], axis=0)
        high, low = split(both)
        c_ref[...] = jnp.concatenate([high, high, low], axis=1)

    sums = {}
    for tile in range(tiles):
        real, imag = (
            jnp.concatenate(
                [
                    x_ref[0, 0, :, part, (g * tiles + tile) * LANES : (g * tiles + tile + 1) * LANES]
                    for g in range(stretches)
                ],
                axis=0,
            )
            for part in range(2)
        )
        real_high, real_low = split(real)
        imag_high, imag_low = split(imag)
        left = jnp.concatenate([real_high, imag_high, real_high, imag_high, real_low, imag_low], axis=1)
        here = covers(tile)
        result = jnp.dot(left, w_ref[tile, :, : len(here) * wide], preferred_element_type=F32)
        for place, r in enumerate(here):
            piece = result[:, place * wide : (place + 1) * wide]
            sums[r] = sums[r] + piece if r in sums else piece
            if (r + 1) * n_ao <= (tile + 1) * LANES:
                done = sums.pop(r)
                for g in range(stretches):
                    t_ref[pl.ds(g * group + r, aux_here, stride=n_ao), :] = done[g * aux_here : (g + 1) * aux_here]

    lane = lax.broadcasted_iota(jnp.int32, (n_occ, wide), 1)
    sign = jnp.where(lane < n_vir, 1.0, -1.0).astype(F32)
    for p in range(0, aux_here, 2):
        both = jnp.concatenate(
            [t_ref[pl.ds(q * n_ao, n_ao), :] for q in (p, p + 1)], axis=1
        )
        high, low = split(both)
        right = jnp.concatenate([high, low, high], axis=0)
        result = jnp.dot(c_ref[...], right, preferred_element_type=F32)
        for q in range(2):
            of_real = result[:n_occ, q * wide : (q + 1) * wide]
            of_imag = result[n_occ:, q * wide : (q + 1) * wide]
            out = of_real + sign * pltpu.roll(of_imag, n_vir, 1)
            for i in range(0, n_occ, 8):
                o_ref[0, pl.ds(i * aux_all + step * aux_here + p + q, 8, stride=aux_all), :] = out[i : i + 8]


def orbitals(ao_blocks, occ_t, vir_t, slot, chosen_rows, kpoint_diff, transfer_label, first_s, count):
    _, _, aux_all, parts, flat = ao_blocks.shape
    n_ao, n_occ, n_vir = occ_t.shape[3], occ_t.shape[2], vir_t.shape[2]
    group = LANES // gcd(n_ao, LANES)
    tiles = n_ao * group // LANES
    aux_here = 8 if aux_all % 16 else 16
    wide = 2 * n_vir
    most = 3

    def block_x(s, c, *refs):
        return (0, first_s + s, c, 0, 0)

    def block_occ(s, c, slot_ref, rows_ref, diff_ref, label_ref):
        return (rows_ref[slot_ref[0], first_s + s], 0, 0, 0)

    def block_vir(s, c, slot_ref, rows_ref, diff_ref, label_ref):
        here = slot_ref[0]
        return (diff_ref[rows_ref[here, first_s + s], label_ref[here]], 0, 0, 0)

    out = pl.pallas_call(
        functools.partial(orbital_kernel, aux_all),
        out_shape=jax.ShapeDtypeStruct((count, n_occ * aux_all, wide), F32),
        grid_spec=pltpu.PrefetchScalarGridSpec(
            num_scalar_prefetch=4,
            grid=(count, aux_all // aux_here),
            in_specs=[
                pl.BlockSpec((1, 1, aux_here, parts, flat), block_x),
                pl.BlockSpec((1, 2, n_occ, n_ao), block_occ),
                pl.BlockSpec((1, 2, n_vir, n_ao), block_vir),
            ],
            out_specs=pl.BlockSpec((1, n_occ * aux_all, wide), lambda s, c, *refs: (s, 0, 0)),
            scratch_shapes=[
                pltpu.VMEM((tiles, 6 * LANES, most * wide), BF16),
                pltpu.VMEM((2 * n_occ, 3 * n_ao), BF16),
                pltpu.VMEM((aux_here * n_ao, wide), F32),
            ],
        ),
        name="orbitals",
    )(slot, chosen_rows, kpoint_diff, transfer_label, ao_blocks, occ_t, vir_t)
    return out.reshape(count, n_occ, aux_all, wide)


def left_kernel(place_ref, *refs):
    n_pieces = place_ref.shape[0]
    pieces, o_ref, held, turned, sem = refs[:n_pieces], *refs[n_pieces:]
    n_here, n_side, aux_each, wide = held.shape[1:]
    copies = [
        pltpu.make_async_copy(piece, held.at[place_ref[m]], sem.at[m]) for m, piece in enumerate(pieces)
    ]
    for copy in copies:
        copy.start()
    for copy in copies:
        copy.wait()
    half = wide // 4
    for s in range(n_here):
        for i in range(n_side):
            whole = held[:, s, i].reshape(n_pieces * aux_each, wide)
            blocks = []
            for c in range(turned.shape[0]):
                turned[c] = jnp.transpose(whole[c * LANES : (c + 1) * LANES], (1, 0))
                picked = [
                    turned[c, pl.ds(part * 2 * half + odd, half, stride=2), :] for part in range(2) for odd in range(2)
                ]
                blocks.append(jnp.concatenate(picked, axis=0))
            rows = jnp.concatenate(blocks, axis=1)
            high, low = split(rows)
            row = (s * n_side + i) * wide
            o_ref[row : row + wide, :] = jnp.concatenate([high, high, low], axis=1)


def left_factor(places, pieces):
    n_s, n_i, aux_each, wide = pieces[0].shape
    depth = len(pieces) * aux_each
    return pl.pallas_call(
        left_kernel,
        out_shape=jax.ShapeDtypeStruct((n_s * n_i * wide, 3 * depth), BF16),
        grid_spec=pltpu.PrefetchScalarGridSpec(
            num_scalar_prefetch=1,
            in_specs=[pl.BlockSpec(memory_space=pl.ANY)] * len(pieces),
            out_specs=pl.BlockSpec(memory_space=pltpu.VMEM),
            scratch_shapes=[
                pltpu.VMEM((len(pieces), n_s, n_i, aux_each, wide), F32),
                pltpu.VMEM((depth // LANES, wide, LANES), F32),
                pltpu.SemaphoreType.DMA((len(pieces),)),
            ],
        ),
        name="left_factor",
    )(places, *pieces)


def pair_kernel(t, hops, n_cores, here_ref, rows_ref, diff_ref, label_ref, left_ref, occ_ref, vir_ref, *refs):
    n_pieces = len(hops)
    pieces = refs[:n_pieces]
    o_ref, held, spread, base, sem = refs[-5:]
    n_blocks, n_j, aux_each, wide = held.shape
    n_s, n_i, per_tile = o_ref.shape[1], o_ref.shape[3], o_ref.shape[4]
    half = wide // 2
    quarter = wide // 4
    step = pl.program_id(0)
    steps_each = per_tile // 2
    slot, aux = here_ref[0], here_ref[1]
    partner = jnp.bitwise_xor(slot, 1)
    n_z = n_blocks // n_cores
    z, core = aux // n_cores, aux % n_cores

    def each_copy(tile, what):
        for piece, (hop, other) in zip(pieces, hops):
            def go(piece=piece, hop=hop, other=other):
                block = (z + hop) * n_cores + (1 - core if other else core)
                rows = pl.ds(tile * per_tile, per_tile)
                copy = pltpu.make_async_copy(piece.at[rows], held.at[block, rows], sem.at[tile])
                copy.start() if what == "start" else copy.wait()

            if hop == 0:
                go()
            else:
                pl.when(z >= -hop if hop < 0 else z + hop < n_z)(go)

    lane = lax.broadcasted_iota(jnp.int32, (quarter, wide), 1)
    first = lane < half
    sign = jnp.where(first, -1.0, 1.0).astype(F32)

    @pl.when(step == 0)
    def _():
        for tile in range(n_j // per_tile):
            each_copy(tile, "start")
        other_row = rows_ref[partner, n_s + t]
        of_b = vir_ref[pl.ds(diff_ref[other_row, label_ref[partner]], 1), :]
        of_b = jnp.concatenate([of_b, of_b], axis=1)
        row = lax.broadcasted_iota(jnp.int32, (quarter, half), 0)
        column = lax.broadcasted_iota(jnp.int32, (quarter, half), 1)
        for s in range(n_s):
            of_a = vir_ref[pl.ds(diff_ref[rows_ref[slot, s], label_ref[slot]], 1), :]
            even = jnp.sum(jnp.where(column == 2 * row, of_a, 0.0), axis=1, keepdims=True)
            odd = jnp.sum(jnp.where(column == 2 * row + 1, of_a, 0.0), axis=1, keepdims=True)
            base[s] = jnp.where(first, even, odd) + of_b

    for tile in range(n_j // per_tile):
        @pl.when(step == tile * steps_each)
        def _():
            each_copy(tile, "wait")

    right = jnp.concatenate(
        [held[:, 2 * step + jj].reshape(n_blocks * aux_each, wide) for jj in range(2)], axis=1
    )
    high, low = split(right)
    right = jnp.concatenate([high, low, high], axis=0)
    other_row = rows_ref[partner, n_s + t]
    for s in range(n_s):
        for i in range(n_i):
            at = (s * n_i + i) * wide
            result = jnp.dot(left_ref[at : at + wide, :], right, preferred_element_type=F32)
            of_i = occ_ref[rows_ref[slot, s], aux * n_i + i]
            for jj in range(2):
                own = result[:, jj * wide : (jj + 1) * wide]
                even = own[:quarter] + sign * pltpu.roll(own[2 * quarter : 3 * quarter], half, 1)
                odd = own[quarter : 2 * quarter] + sign * pltpu.roll(own[3 * quarter :], half, 1)
                of_j = occ_ref[other_row, 2 * step + jj]
                inverse = 1.0 / ((of_i + of_j) - base[s])
                real = jnp.where(first, even, pltpu.roll(odd, half, 1)) * inverse
                imag = jnp.where(first, pltpu.roll(even, half, 1), odd) * inverse
                slot_j = lax.rem(2 * step, per_tile) + jj
                spread[0, s, i, pl.ds(slot_j, quarter, stride=per_tile), :] = real
                spread[1, s, i, pl.ds(slot_j, quarter, stride=per_tile), :] = imag

    @pl.when(lax.rem(step, steps_each) == steps_each - 1)
    def _():
        for part in range(2):
            for s in range(n_s):
                for i in range(n_i):
                    for k in range(quarter):
                        o_ref[part, s, 0, i, :, k * wide : (k + 1) * wide] = spread[
                            part, s, i, k * per_tile : (k + 1) * per_tile, :
                        ]


def pair_products(t, here, tables, left, occ_energy, vir_energy, pieces, hops, n_cores, n_s, n_t, n_i, before):
    n_j, aux_each, wide = pieces[0].shape
    n_blocks = left.shape[1] // (3 * aux_each)
    per_tile = 8
    quarter = wide // 4
    flat = (wide // 2) ** 2
    steps = n_j // 2
    any_spec = pl.BlockSpec(memory_space=pl.ANY)
    extra = [] if before is None else [before]
    return pl.pallas_call(
        functools.partial(pair_kernel, t, hops, n_cores),
        out_shape=jax.ShapeDtypeStruct((2, n_s, n_t, n_i, n_j, flat), F32),
        grid_spec=pltpu.PrefetchScalarGridSpec(
            num_scalar_prefetch=4,
            grid=(steps,),
            in_specs=[
                pl.BlockSpec(left.shape, lambda p, *refs: (0, 0)),
                pl.BlockSpec(memory_space=pltpu.SMEM),
                pl.BlockSpec(vir_energy.shape, lambda p, *refs: (0, 0)),
            ]
            + [any_spec] * (len(pieces) + len(extra)),
            out_specs=pl.BlockSpec(
                (2, n_s, 1, n_i, per_tile, flat), lambda p, *refs: (0, 0, t, 0, p // (per_tile // 2), 0)
            ),
            scratch_shapes=[
                pltpu.VMEM((n_blocks, n_j, aux_each, wide), F32),
                pltpu.VMEM((2, n_s, n_i, quarter * per_tile, wide), F32),
                pltpu.VMEM((n_s, quarter, wide), F32),
                pltpu.SemaphoreType.DMA((n_j // per_tile,)),
            ],
        ),
        input_output_aliases={} if before is None else {7 + len(pieces): 0},
        name="pair_products",
    )(here, *tables, left, occ_energy, vir_energy, *pieces, *extra)


def swap_with(value, axis, mask):
    return lax.ppermute(value, axis, [(d, d ^ mask) for d in range(lax.axis_size(axis))])


def along_line(value, n_cores, sources, move, flip=False):
    pairs = []
    for z in sources:
        for core in range(n_cores):
            pairs.append((z * n_cores + core, (z + move) * n_cores + (core ^ flip)))
    return lax.ppermute(value, "aux", pairs)


def gather_partner(own, n_cores):
    n_z = lax.axis_size("aux") // n_cores
    pieces, hops = [own], [(0, False)]
    every = range(n_z)
    pieces.append(along_line(own, n_cores, every, 0, True))
    hops.append((0, True))
    right = left = own
    for k in range(1, n_z):
        right = along_line(right, n_cores, range(k - 1, n_z - 1), 1)
        left = along_line(left, n_cores, range(1, n_z - k + 1), -1)
        pieces += [right, left]
        hops += [(-k, False), (k, False)]
        pieces.append(along_line(right, n_cores, range(k, n_z), 0, True))
        pieces.append(along_line(left, n_cores, range(0, n_z - k), 0, True))
        hops += [(-k, True), (k, True)]
    return pieces, hops


def per_device(
    ao_blocks, occ_coef, vir_coef, occ_energy, vir_energy, kpoint_diff, transfer_label, chosen_rows
):
    n_cores = 2
    slot, aux = lax.axis_index("pb"), lax.axis_index("aux")
    n_aux = lax.axis_size("aux")
    n_s = n_t = chosen_rows.shape[1] // 2
    here = jnp.stack([slot, aux]).astype(jnp.int32)
    tables = (chosen_rows, kpoint_diff, transfer_label)
    occ_t, vir_t = jnp.swapaxes(occ_coef, 2, 3), jnp.swapaxes(vir_coef, 2, 3)
    turn = functools.partial(orbitals, ao_blocks, occ_t, vir_t, here, *tables)

    ki_side = turn(0, n_s)
    kj_sides = [turn(n_s + t, 1)[0] for t in range(n_t)]
    n_occ = ki_side.shape[1]
    n_i = n_occ // n_aux

    ki_pieces = []
    for m in range(n_aux):
        rows = lax.dynamic_slice_in_dim(ki_side, jnp.bitwise_xor(aux, m) * n_i, n_i, 1)
        ki_pieces.append(swap_with(rows, "aux", m) if m else rows)
    places = jnp.bitwise_xor(aux, jnp.arange(n_aux, dtype=jnp.int32)).astype(jnp.int32)

    result = None
    left = None
    gathered = []
    for t in range(n_t):
        own = swap_with(kj_sides[t], "pb", 1)
        gathered.append(gather_partner(own, n_cores))
    left = left_factor(places, ki_pieces)
    for t in range(n_t):
        pieces, hops = gathered[t]
        result = pair_products(
            t, here, tables, left, occ_energy, vir_energy, pieces, hops, n_cores, n_s, n_t, n_i, result
        )
    return result[None]


def solution(mesh):
    in_specs = (P("pb", None, "aux", None, None), P(), P(), P(), P(), P(), P(), P())
    out_specs = P("pb", None, None, None, "aux", None, None)
    return jax.shard_map(
        per_device, mesh=mesh, in_specs=in_specs, out_specs=out_specs, check_vma=False
    )
```

```python
import functools

import jax
import jax.numpy as jnp
from jax import lax
from jax.experimental import pallas as pl
from jax.experimental.pallas import tpu as pltpu
from jax.sharding import PartitionSpec as P


LANES = 128
F32 = jnp.float32
BF16 = jnp.bfloat16


def gcd(a, b):
    while b:
        a, b = b, a % b
    return a


def split(value):
    high = value.astype(BF16)
    low = (value - high.astype(F32)).astype(BF16)
    return high, low


def orbital_kernel(
    first_s,
    slot_ref,
    rows_ref,
    diff_ref,
    label_ref,
    x_hbm,
    occ_ref,
    vir_ref,
    o_ref,
    x_ref,
    w_ref,
    c_ref,
    t_ref,
    sem,
):
    n_ao = occ_ref.shape[3]
    n_occ = occ_ref.shape[2]
    n_vir = vir_ref.shape[2]
    group = LANES // gcd(n_ao, LANES)
    tiles = n_ao * group // LANES
    aux_all = x_hbm.shape[2]
    aux_here = x_ref.shape[3]
    n_steps = x_ref.shape[1]
    stretches = n_ao // group
    wide = 2 * n_vir
    row, step = pl.program_id(0), pl.program_id(1)

    def fetch(s, c, part):
        return pltpu.make_async_copy(
            x_hbm.at[0, first_s + s, pl.ds(c * aux_here, aux_here), part], x_ref.at[s, c, part], sem.at[s, c, part]
        )

    @pl.when(jnp.logical_and(row == 0, step == 0))
    def _():
        for s in range(x_ref.shape[0]):
            for c in range(n_steps):
                for part in range(2):
                    fetch(s, c, part).start()

    def covers(tile):
        return [r for r in range(group) if r * n_ao < (tile + 1) * LANES and (r + 1) * n_ao > tile * LANES]

    @pl.when(step == 0)
    def _():
        vir_real = jnp.transpose(vir_ref[0, 0], (1, 0))
        vir_imag = jnp.transpose(vir_ref[0, 1], (1, 0))
        of_real = jnp.concatenate([vir_real, vir_imag], axis=1)
        of_imag = jnp.concatenate([-vir_imag, vir_real], axis=1)
        w_ref[...] = jnp.zeros_like(w_ref)
        for part, both in enumerate((of_real, of_imag)):
            high, low = split(both)
            for tile in range(tiles):
                for place, r in enumerate(covers(tile)):
                    start = max(0, r * n_ao - tile * LANES)
                    stop = min(LANES, (r + 1) * n_ao - tile * LANES)
                    begin = tile * LANES + start - r * n_ao
                    for kind, piece in enumerate((high, low, high)):
                        row = kind * 2 * LANES + part * LANES + start
                        w_ref[tile, row : row + stop - start, place * wide : (place + 1) * wide] = piece[
                            begin : begin + stop - start
                        ]
        both = jnp.concatenate([occ_ref[0, 0], occ_ref[0, 1]], axis=0)
        high, low = split(both)
        c_ref[...] = jnp.concatenate([high, high, low], axis=1)

    for part in range(2):
        fetch(row, step, part).wait()
    sums = {}
    for tile in range(tiles):
        real, imag = (
            jnp.concatenate(
                [
                    x_ref[row, step, part, :, (g * tiles + tile) * LANES : (g * tiles + tile + 1) * LANES]
                    for g in range(stretches)
                ],
                axis=0,
            )
            for part in range(2)
        )
        real_high, real_low = split(real)
        imag_high, imag_low = split(imag)
        left = jnp.concatenate([real_high, imag_high, real_high, imag_high, real_low, imag_low], axis=1)
        here = covers(tile)
        result = jnp.dot(left, w_ref[tile, :, : len(here) * wide], preferred_element_type=F32)
        for place, r in enumerate(here):
            piece = result[:, place * wide : (place + 1) * wide]
            sums[r] = sums[r] + piece if r in sums else piece
            if (r + 1) * n_ao <= (tile + 1) * LANES:
                done = sums.pop(r)
                for g in range(stretches):
                    t_ref[pl.ds(g * group + r, aux_here, stride=n_ao), :] = done[g * aux_here : (g + 1) * aux_here]

    lane = lax.broadcasted_iota(jnp.int32, (n_occ, wide), 1)
    sign = jnp.where(lane < n_vir, 1.0, -1.0).astype(F32)
    for p in range(0, aux_here, 2):
        both = jnp.concatenate(
            [t_ref[pl.ds(q * n_ao, n_ao), :] for q in (p, p + 1)], axis=1
        )
        high, low = split(both)
        right = jnp.concatenate([high, low, high], axis=0)
        result = jnp.dot(c_ref[...], right, preferred_element_type=F32)
        for q in range(2):
            of_real = result[:n_occ, q * wide : (q + 1) * wide]
            of_imag = result[n_occ:, q * wide : (q + 1) * wide]
            out = of_real + sign * pltpu.roll(of_imag, n_vir, 1)
            for i in range(0, n_occ, 8):
                o_ref[0, pl.ds(i * aux_all + step * aux_here + p + q, 8, stride=aux_all), :] = out[i : i + 8]


def orbitals(ao_blocks, occ_t, vir_t, slot, chosen_rows, kpoint_diff, transfer_label, first_s, count):
    _, _, aux_all, parts, flat = ao_blocks.shape
    n_ao, n_occ, n_vir = occ_t.shape[3], occ_t.shape[2], vir_t.shape[2]
    group = LANES // gcd(n_ao, LANES)
    tiles = n_ao * group // LANES
    aux_here = next(n for n in (40, 16, 8) if aux_all % n == 0)
    wide = 2 * n_vir
    most = 3

    def block_occ(s, c, slot_ref, rows_ref, diff_ref, label_ref):
        return (rows_ref[slot_ref[0], first_s + s], 0, 0, 0)

    def block_vir(s, c, slot_ref, rows_ref, diff_ref, label_ref):
        here = slot_ref[0]
        return (diff_ref[rows_ref[here, first_s + s], label_ref[here]], 0, 0, 0)

    out = pl.pallas_call(
        functools.partial(orbital_kernel, first_s),
        out_shape=jax.ShapeDtypeStruct((count, n_occ * aux_all, wide), F32),
        grid_spec=pltpu.PrefetchScalarGridSpec(
            num_scalar_prefetch=4,
            grid=(count, aux_all // aux_here),
            in_specs=[
                pl.BlockSpec(memory_space=pl.ANY),
                pl.BlockSpec((1, 2, n_occ, n_ao), block_occ),
                pl.BlockSpec((1, 2, n_vir, n_ao), block_vir),
            ],
            out_specs=pl.BlockSpec((1, n_occ * aux_all, wide), lambda s, c, *refs: (s, 0, 0)),
            scratch_shapes=[
                pltpu.VMEM((count, aux_all // aux_here, parts, aux_here, flat), F32),
                pltpu.VMEM((tiles, 6 * LANES, most * wide), BF16),
                pltpu.VMEM((2 * n_occ, 3 * n_ao), BF16),
                pltpu.VMEM((aux_here * n_ao, wide), F32),
                pltpu.SemaphoreType.DMA((count, aux_all // aux_here, parts)),
            ],
        ),
        cost_estimate=pl.CostEstimate(
            flops=count * aux_all * 12 * n_ao * n_occ * n_ao * 64, bytes_accessed=count * aux_all * parts * flat * 4 * 8,
            transcendentals=0,
        ),
        name="orbitals",
    )(slot, chosen_rows, kpoint_diff, transfer_label, ao_blocks, occ_t, vir_t)
    return out.reshape(count, n_occ, aux_all, wide)


def left_kernel(place_ref, *refs):
    n_pieces = place_ref.shape[0]
    pieces, o_ref, held, turned, sem = refs[:n_pieces], *refs[n_pieces:]
    n_here, n_side, aux_each, wide = held.shape[1:]
    copies = [
        pltpu.make_async_copy(piece, held.at[place_ref[m]], sem.at[m]) for m, piece in enumerate(pieces)
    ]
    for copy in copies:
        copy.start()
    for copy in copies:
        copy.wait()
    half = wide // 4
    for s in range(n_here):
        for i in range(n_side):
            whole = held[:, s, i].reshape(n_pieces * aux_each, wide)
            blocks = []
            for c in range(turned.shape[0]):
                turned[c] = jnp.transpose(whole[c * LANES : (c + 1) * LANES], (1, 0))
                picked = [
                    turned[c, pl.ds(part * 2 * half + odd, half, stride=2), :] for part in range(2) for odd in range(2)
                ]
                blocks.append(jnp.concatenate(picked, axis=0))
            rows = jnp.concatenate(blocks, axis=1)
            high, low = split(rows)
            row = (s * n_side + i) * wide
            o_ref[row : row + wide, :] = jnp.concatenate([high, high, low], axis=1)


def left_factor(places, pieces):
    n_s, n_i, aux_each, wide = pieces[0].shape
    depth = len(pieces) * aux_each
    return pl.pallas_call(
        left_kernel,
        out_shape=jax.ShapeDtypeStruct((n_s * n_i * wide, 3 * depth), BF16),
        grid_spec=pltpu.PrefetchScalarGridSpec(
            num_scalar_prefetch=1,
            in_specs=[pl.BlockSpec(memory_space=pl.ANY)] * len(pieces),
            out_specs=pl.BlockSpec(memory_space=pltpu.VMEM),
            scratch_shapes=[
                pltpu.VMEM((len(pieces), n_s, n_i, aux_each, wide), F32),
                pltpu.VMEM((depth // LANES, wide, LANES), F32),
                pltpu.SemaphoreType.DMA((len(pieces),)),
            ],
        ),
        cost_estimate=pl.CostEstimate(flops=10**9, bytes_accessed=12 * 10**6, transcendentals=0),
        name="left_factor",
    )(places, *pieces)


def pair_kernel(t, hops, n_cores, here_ref, rows_ref, diff_ref, label_ref, left_ref, occ_ref, vir_ref, *refs):
    n_pieces = len(hops)
    pieces = refs[:n_pieces]
    o_ref, held, product, spread, base, sem = refs[-6:]
    n_blocks, n_j, aux_each, wide = held.shape
    n_s, n_i, per_tile = o_ref.shape[1], o_ref.shape[3], o_ref.shape[4]
    half = wide // 2
    quarter = wide // 4
    step = pl.program_id(0)
    steps_each = per_tile // 2
    slot, aux = here_ref[0], here_ref[1]
    partner = jnp.bitwise_xor(slot, 1)
    n_z = n_blocks // n_cores
    z, core = aux // n_cores, aux % n_cores

    def each_copy(tile, what):
        for piece, (reach, other) in zip(pieces, hops):
            here_z = sorted(reach)
            chip = reach[here_z[0]]
            within = z == here_z[0]
            for at_z in here_z[1:]:
                chip = jnp.where(z == at_z, reach[at_z], chip)
                within = jnp.logical_or(within, z == at_z)

            def go(piece=piece, chip=chip, other=other):
                block = chip * n_cores + (1 - core if other else core)
                rows = pl.ds(tile * per_tile, per_tile)
                copy = pltpu.make_async_copy(piece.at[rows], held.at[block, rows], sem.at[tile])
                copy.start() if what == "start" else copy.wait()

            go() if len(here_z) == n_z else pl.when(within)(go)

    lane = lax.broadcasted_iota(jnp.int32, (quarter, wide), 1)
    first = lane < half
    sign = jnp.where(first, -1.0, 1.0).astype(F32)

    @pl.when(step == 0)
    def _():
        for tile in range(n_j // per_tile):
            each_copy(tile, "start")
        other_row = rows_ref[partner, n_s + t]
        of_b = vir_ref[pl.ds(diff_ref[other_row, label_ref[partner]], 1), :]
        of_b = jnp.concatenate([of_b, of_b], axis=1)
        row = lax.broadcasted_iota(jnp.int32, (quarter, half), 0)
        column = lax.broadcasted_iota(jnp.int32, (quarter, half), 1)
        for s in range(n_s):
            of_a = vir_ref[pl.ds(diff_ref[rows_ref[slot, s], label_ref[slot]], 1), :]
            even = jnp.sum(jnp.where(column == 2 * row, of_a, 0.0), axis=1, keepdims=True)
            odd = jnp.sum(jnp.where(column == 2 * row + 1, of_a, 0.0), axis=1, keepdims=True)
            base[s] = jnp.where(first, even, odd) + of_b

    for tile in range(n_j // per_tile):
        @pl.when(step == tile * steps_each)
        def _():
            each_copy(tile, "wait")

    other_row = rows_ref[partner, n_s + t]
    n_steps = n_j // 2

    def multiply():
        right = jnp.concatenate(
            [held[:, 2 * step + jj].reshape(n_blocks * aux_each, wide) for jj in range(2)], axis=1
        )
        high, low = split(right)
        right = jnp.concatenate([high, low, high], axis=0)
        product[...] = jnp.dot(left_ref[...], right, preferred_element_type=F32)

    def finish():
        for s in range(n_s):
            for i in range(n_i):
                at = (s * n_i + i) * wide
                of_i = occ_ref[rows_ref[slot, s], aux * n_i + i]
                for jj in range(2):
                    own = [
                        product[at + q * quarter : at + (q + 1) * quarter, jj * wide : (jj + 1) * wide] for q in range(4)
                    ]
                    even = own[0] + sign * pltpu.roll(own[2], half, 1)
                    odd = own[1] + sign * pltpu.roll(own[3], half, 1)
                    of_j = occ_ref[other_row, 2 * (step - 1) + jj]
                    inverse = 1.0 / ((of_i + of_j) - base[s])
                    real = jnp.where(first, even, pltpu.roll(odd, half, 1)) * inverse
                    imag = jnp.where(first, pltpu.roll(even, half, 1), odd) * inverse
                    slot_j = lax.rem(2 * (step - 1), per_tile) + jj
                    spread[0, s, i, pl.ds(slot_j, quarter, stride=per_tile), :] = real
                    spread[1, s, i, pl.ds(slot_j, quarter, stride=per_tile), :] = imag

    pl.when(step == 0)(multiply)

    @pl.when(jnp.logical_and(step > 0, step < n_steps))
    def _():
        finish()
        multiply()

    pl.when(step == n_steps)(finish)

    @pl.when(jnp.logical_and(step > 0, lax.rem(step, steps_each) == 0))
    def _():
        for part in range(2):
            for s in range(n_s):
                for i in range(n_i):
                    for k in range(quarter):
                        o_ref[part, s, 0, i, :, k * wide : (k + 1) * wide] = spread[
                            part, s, i, k * per_tile : (k + 1) * per_tile, :
                        ]


def pair_products(t, here, tables, left, occ_energy, vir_energy, pieces, hops, n_cores, n_s, n_t, n_i, before):
    n_j, aux_each, wide = pieces[0].shape
    n_blocks = left.shape[1] // (3 * aux_each)
    per_tile = 8
    quarter = wide // 4
    flat = (wide // 2) ** 2
    steps = n_j // 2
    any_spec = pl.BlockSpec(memory_space=pl.ANY)
    extra = [] if before is None else [before]
    return pl.pallas_call(
        functools.partial(pair_kernel, t, hops, n_cores),
        out_shape=jax.ShapeDtypeStruct((2, n_s, n_t, n_i, n_j, flat), F32),
        grid_spec=pltpu.PrefetchScalarGridSpec(
            num_scalar_prefetch=4,
            grid=(steps + 1,),
            in_specs=[
                pl.BlockSpec(left.shape, lambda p, *refs: (0, 0)),
                pl.BlockSpec(memory_space=pltpu.SMEM),
                pl.BlockSpec(vir_energy.shape, lambda p, *refs: (0, 0)),
            ]
            + [any_spec] * (len(pieces) + len(extra)),
            out_specs=pl.BlockSpec(
                (2, n_s, 1, n_i, per_tile, flat), lambda p, *refs: (0, 0, t, 0, jnp.maximum(p - 1, 0) // (per_tile // 2), 0)
            ),
            scratch_shapes=[
                pltpu.VMEM((n_blocks, n_j, aux_each, wide), F32),
                pltpu.VMEM((left.shape[0], 2 * wide), F32),
                pltpu.VMEM((2, n_s, n_i, quarter * per_tile, wide), F32),
                pltpu.VMEM((n_s, quarter, wide), F32),
                pltpu.SemaphoreType.DMA((n_j // per_tile,)),
            ],
        ),
        input_output_aliases={} if before is None else {7 + len(pieces): 0},
        cost_estimate=pl.CostEstimate(
            flops=6 * left.shape[0] * left.shape[1] * n_j * wide, bytes_accessed=40 * 10**6, transcendentals=0
        ),
        name="pair_products",
    )(here, *tables, left, occ_energy, vir_energy, *pieces, *extra)


def swap_with(value, axis, mask):
    return lax.ppermute(value, axis, [(d, d ^ mask) for d in range(lax.axis_size(axis))])


def along_line(value, n_cores, sources, move, flip=False):
    pairs = []
    for z in sources:
        for core in range(n_cores):
            pairs.append((z * n_cores + core, (z + move) * n_cores + (core ^ flip)))
    return lax.ppermute(value, "aux", pairs)


def gather_partner(own, n_cores):
    n_z = lax.axis_size("aux") // n_cores
    pieces, hops = [], []

    def keep(value, reach):
        pieces.append(value)
        hops.append((reach, False))
        pieces.append(along_line(value, n_cores, sorted(reach), 0, True))
        hops.append((reach, True))

    right = left = own
    keep(own, {z: z for z in range(n_z)})
    for k in range(1, n_z):
        to_right, to_left = range(k - 1, n_z - 1), range(1, n_z - k + 1)
        from_left = {z: z - k for z in range(k, n_z)}
        from_right = {z: z + k for z in range(n_z - k)}
        if right is left and k > 1:
            pairs = [(z, z + 1) for z in to_right] + [(z, z - 1) for z in to_left]
            right = left = lax.ppermute(
                right, "aux", [(a * n_cores + c, b * n_cores + c) for a, b in pairs for c in range(n_cores)]
            )
            keep(right, from_left | from_right)
            continue
        right = along_line(right, n_cores, to_right, 1)
        left = along_line(left, n_cores, to_left, -1)
        if not from_left.keys() & from_right.keys():
            right = left = right + left
            keep(right, from_left | from_right)
        else:
            keep(right, from_left)
            keep(left, from_right)
    return pieces, hops


def per_device(
    ao_blocks, occ_coef, vir_coef, occ_energy, vir_energy, kpoint_diff, transfer_label, chosen_rows
):
    n_cores = 2
    slot, aux = lax.axis_index("pb"), lax.axis_index("aux")
    n_aux = lax.axis_size("aux")
    n_s = n_t = chosen_rows.shape[1] // 2
    here = jnp.stack([slot, aux]).astype(jnp.int32)
    tables = (chosen_rows, kpoint_diff, transfer_label)
    occ_t, vir_t = jnp.swapaxes(occ_coef, 2, 3), jnp.swapaxes(vir_coef, 2, 3)

    def turn(place, first_s, count):
        return orbitals(ao_blocks, occ_t, vir_t, place, *tables, first_s, count)


    def kj_side(t, place):
        return turn(place, n_s + t, 1)[0]

    def cross(value):
        own = swap_with(value, "pb", 1)
        return gather_partner(own, n_cores)

    first = kj_side(0, here)
    after, first = lax.optimization_barrier((here, first))
    gathered = [cross(first)]
    ki_side = turn(after, 0, n_s)
    n_i = ki_side.shape[1] // n_aux
    rows_of = [
        lax.dynamic_slice_in_dim(ki_side, jnp.bitwise_xor(aux, m) * n_i, n_i, 1) for m in range(n_aux)
    ]
    places = jnp.bitwise_xor(aux, jnp.arange(n_aux, dtype=jnp.int32)).astype(jnp.int32)
    after, places, *rows_of = lax.optimization_barrier((here, places, *rows_of))
    ki_pieces = rows_of[:1]
    for m in range(1, n_aux):
        ki_pieces.append(swap_with(rows_of[m], "aux", m))
    for t in range(1, n_t):
        gathered.append(cross(kj_side(t, after)))
    left = left_factor(places, ki_pieces)
    result = None
    for t in range(n_t):
        pieces, hops = gathered[t]
        result = pair_products(
            t, here, tables, left, occ_energy, vir_energy, pieces, hops, n_cores, n_s, n_t, n_i, result
        )
    return result[None]


def solution(mesh):
    in_specs = (P("pb", None, "aux", None, None), P(), P(), P(), P(), P(), P(), P())
    out_specs = P("pb", None, None, None, "aux", None, None)

    return jax.shard_map(per_device, mesh=mesh, in_specs=in_specs, out_specs=out_specs, check_vma=False)
```
